32 devices in a mesh: tm: 16 (over z, y, x), col: 2 (over core).
Axes of the slice: x: 2, y: 2, z: 4, core: 2. Of those that a mesh axis runs over, the one named last changes fastest.
Arguments:
- diagonal_blocks: float32 [32, 512, 512], P('tm', 'col'), as said below
- upper_blocks: float32 [32, 512, 512], P('tm', 'col')
- right_sides: float32 [32, 512, 512], P('tm', 'col'), may hold values from -6 to 6
Outputs:
- reduced_blocks: float32 [32, 512, 512], P('tm', 'col')
- reduced_uppers: float32 [32, 512, 512], P('tm', 'col')
- reduced_sources: float32 [32, 512, 512], P('tm', 'col')
The draws below stay inside these ranges and needn't reach their ends.
Inputs may be any that keep to these rules, and one draw needn't show every extreme that they name: `diagonal_blocks`: every block is symmetric, and the block-tridiagonal matrix built from these blocks and upper_blocks is positive definite.
All inputs are finite; a program needn't handle non-finite values.
Results may differ from the reference program's by a relative error of at most 0.0001.
Values sent between devices are 32-bit elements; how exact they have to be, the bound alone decides.
A program may use at most 64 MiB of HBM per device.

```python
import jax
import jax.numpy as jnp
from jax import lax

MODES = 512
SOURCES = 512
LEVELS = 2
ROWS = 32


def coupling_factor(key):
    phi_key = jax.random.fold_in(key, 11)
    entries = jnp.clip(jax.random.normal(phi_key, (ROWS, MODES, MODES), jnp.float32), -6.0, 6.0)
    return entries * (2.0 / jnp.sqrt(1.0 * MODES))


def draw_diagonal_blocks(key, part):
    factor = coupling_factor(key)
    dense_key = jax.random.fold_in(key, 23)
    height_key = jax.random.fold_in(key, 37)
    dense = jnp.clip(jax.random.normal(dense_key, (ROWS, MODES, MODES), jnp.float32), -6.0, 6.0)
    dense = dense * (2.0 / jnp.sqrt(1.0 * MODES))
    total = jnp.einsum('nab,ncb->nac', factor, factor, precision=lax.Precision.HIGHEST) + jnp.einsum('nab,ncb->nac', dense, dense, precision=lax.Precision.HIGHEST)
    total = 0.5 * (total + jnp.swapaxes(total, 1, 2))
    heights = jnp.exp(jax.random.uniform(height_key, (ROWS, MODES), jnp.float32, jnp.log(3.0), jnp.log(9.0)))
    return total + heights[:, :, None] * jnp.eye(MODES, dtype=jnp.float32)


def draw_upper_blocks(key, part):
    return -jnp.swapaxes(coupling_factor(key), 1, 2)


def block_levels(own_key, shape, pieces, least, top_value):
    gain = 1.0
    for axis_at, parts in pieces:
        draws = jax.random.uniform(jax.random.fold_in(jax.random.fold_in(own_key, 6), axis_at), (parts,), jnp.float32, least / len(pieces), top_value / len(pieces))
        gain = gain * jnp.repeat(jnp.exp(draws), shape[axis_at] // parts).reshape((-1,) + (1,) * (len(shape) - 1 - axis_at))
    return gain


def noise(own_key, dims, width, most, pieces=(), kind=jnp.bfloat16):
    result = jax.random.normal(own_key, dims, jnp.float32) * width
    if len(pieces) > 0:
        result = block_levels(own_key, dims, pieces, -0.22, 0.18) * result
    return jnp.clip(result, min=-most, max=most).astype(kind)


def setup_inputs(seed: int = 0) -> dict:
    streams_of = jax.random.split(jax.random.key(seed), 4)
    diagonal_blocks = draw_diagonal_blocks(jax.random.fold_in(streams_of[3], 71), 0)
    upper_blocks = draw_upper_blocks(jax.random.fold_in(streams_of[3], 71), 0)
    right_sides = noise(streams_of[2], (ROWS, SOURCES, MODES), 1.0, 6.0, ((0, 16), (1, 2)), jnp.float32)
    return dict(diagonal_blocks=diagonal_blocks, upper_blocks=upper_blocks, right_sides=right_sides)


HIGHEST = lax.Precision.HIGHEST

def solve_right(factor, values, transposed):
    return lax.linalg.triangular_solve(factor, values, left_side=False, lower=True, transpose_a=transposed)

def apply_inverse(factor, values):
    return solve_right(factor, solve_right(factor, values, True), False)

def product(pattern, left_operand, right_operand):
    return jnp.einsum(pattern, left_operand, right_operand, precision=HIGHEST)

def eliminate(pivot, coupling, onward, sources):
    factor = lax.linalg.cholesky(pivot)
    scaled = apply_inverse(factor, coupling)
    solved = apply_inverse(factor, sources)
    turned = apply_inverse(factor, jnp.swapaxes(onward, 1, 2))
    left_block = -product('nab,ncb->nac', scaled, coupling)
    left_source = -product('nkb,ncb->nkc', solved, coupling)
    right_block = -product('nab,nbc->nac', turned, onward)
    right_upper = -product('nab,nbc->nac', scaled, onward)
    right_source = -product('nkb,nbc->nkc', solved, onward)
    return (left_block, left_source, right_block, right_upper, right_source)

def shifted(values):
    return jnp.concatenate([jnp.zeros_like(values[:1]), values[:-1]], axis=0)

def reference(diagonal_blocks, upper_blocks, right_sides):
    blocks = diagonal_blocks
    uppers = upper_blocks
    sources = right_sides
    for level_index in range(LEVELS):
        stride = 2 ** level_index
        active_block = blocks[::stride]
        active_upper = uppers[::stride]
        active_source = sources[::stride]
        onward = jnp.concatenate([active_upper[2::2], jnp.zeros_like(active_upper[:1])], axis=0)
        left_block, left_source, right_block, right_upper, right_source = eliminate(active_block[1::2], active_upper[1::2], onward, active_source[1::2])
        kept_block = active_block[0::2] + left_block + shifted(right_block)
        kept_upper = jnp.concatenate([active_upper[:1], right_upper[:-1]], axis=0)
        kept_source = active_source[0::2] + left_source + shifted(right_source)
        blocks = blocks.at[::2 * stride].set(kept_block)
        uppers = uppers.at[::2 * stride].set(kept_upper)
        sources = sources.at[::2 * stride].set(kept_source)
    return (blocks, uppers, sources)
```

```python
import functools

import jax
import jax.numpy as jnp
from jax import lax
from jax.experimental import pallas as pl
from jax.experimental.pallas import tpu as pltpu
from jax.sharding import PartitionSpec as P

LEVELS = 2
TILE = 128
PANEL = 8
F32 = jnp.float32
BF16 = jnp.bfloat16


def split(values):
    high = values.astype(BF16)
    return high, (values - high.astype(F32)).astype(BF16)


def dot_parts(left, right, dims):
    def one(a, b):
        return lax.dot_general(a, b, (dims, ((), ())), preferred_element_type=F32)

    return one(left[0], right[0]) + (one(left[0], right[1]) + one(left[1], right[0]))


def dot3(left, right, dims=((1,), (0,))):
    return dot_parts(split(left), split(right), dims)


def dot6(left, right):
    return jnp.dot(left, right, precision=lax.Precision.HIGHEST, preferred_element_type=F32)


def panel_step(a):
    size = a.shape[0]
    lanes = lax.broadcasted_iota(jnp.int32, (PANEL, size), 1)
    subs = lax.broadcasted_iota(jnp.int32, (PANEL, size), 0)
    cols = [jnp.broadcast_to(a[:, i : i + 1], (size, size)) for i in range(PANEL)]
    rows = [
        jnp.where(
            lanes < PANEL,
            jnp.where(lanes == i, 1.0, 0.0),
            jnp.broadcast_to(a[i : i + 1, :], (PANEL, size)),
        )
        for i in range(PANEL)
    ]
    s = [
        [jnp.broadcast_to(cols[j][i : i + 1, :], (PANEL, size)) if j >= i else None for j in range(PANEL)]
        for i in range(PANEL)
    ]
    scale = [None] * PANEL
    low = {}
    for k in range(PANEL):
        scale[k] = 1.0 / s[k][k]
        for i in range(k + 1, PANEL):
            low[i, k] = s[k][i] * scale[k]
            for j in range(i, PANEL):
                s[i][j] = s[i][j] - low[i, k] * s[k][j]
            rows[i] = rows[i] - low[i, k] * rows[k]
    for k in range(PANEL - 1, -1, -1):
        rows[k] = rows[k] * scale[k]
        for i in range(k):
            pass
    for k in range(PANEL - 1, 0, -1):
        for i in range(k):
            rows[i] = rows[i] - low[k, i] * rows[k]
    solved = rows[0]
    for i in range(1, PANEL):
        solved = jnp.where(subs == i, rows[i], solved)
    pieces = []
    for g in range(1, size // PANEL):
        at = slice(g * PANEL, (g + 1) * PANEL)
        rest = jnp.where(lanes < PANEL, 0.0, a[at])
        first = cols[0][at] * rows[0]
        second = cols[1][at] * rows[1]
        for i in range(2, PANEL, 2):
            first = first + cols[i][at] * rows[i]
            second = second + cols[i + 1][at] * rows[i + 1]
        pieces.append(rest - (first + second))
    pieces.append(solved)
    return pltpu.roll(jnp.concatenate(pieces, axis=0), size - PANEL, axis=1)


def inverse_kernel(at_ref, own_ref, other_ref, zown_ref, zother_ref, s_ref, tile_ref):
    half = own_ref.shape[0]
    size = s_ref.shape[0]
    own_at = pl.ds(pl.multiple_of(at_ref[0] * half, half), half)
    other_at = pl.ds(pl.multiple_of((1 - at_ref[0]) * half, half), half)
    s_ref[own_at, :] = own_ref[...]
    s_ref[other_at, :] = other_ref[...]
    for k in range(0, size, TILE):
        at = slice(k, k + TILE)
        tile_ref[...] = s_ref[at, at]

        @pl.loop(0, TILE // PANEL)
        def _(_step):
            tile_ref[...] = panel_step(tile_ref[...])

        inverse = tile_ref[...]
        row = dot6(inverse, s_ref[at, :])
        s_ref[at, :] = row
        s_ref[at, at] = inverse
        for r in range(0, size, TILE):
            if r != k:
                rat = slice(r, r + TILE)
                column = s_ref[rat, at]
                s_ref[rat, at] = jnp.zeros((TILE, TILE), F32)
                s_ref[rat, :] = s_ref[rat, :] - dot6(column, s_ref[at, :])
    zown_ref[...] = s_ref[own_at, :]
    zother_ref[...] = s_ref[other_at, :]


SMEM = pl.BlockSpec(memory_space=pltpu.SMEM)
VMEM = pl.BlockSpec(memory_space=pltpu.VMEM)


def call(kernel, marks, operands, outs, scratch, flops, name):
    moved = 4 * sum(x.size for x in operands)
    return pl.pallas_call(
        kernel,
        out_shape=[jax.ShapeDtypeStruct(shape, F32) for shape in outs],
        in_specs=[SMEM] + [VMEM] * len(operands),
        out_specs=[VMEM] * len(outs),
        scratch_shapes=[pltpu.VMEM(shape, F32) for shape in scratch],
        cost_estimate=pl.CostEstimate(flops=flops, bytes_accessed=moved, transcendentals=0),
        compiler_params=pltpu.CompilerParams(vmem_limit_bytes=40 * 2**20),
        name=name,
    )(marks, *operands)


def inverse(marks, own, other):
    half, size = own.shape
    return call(
        inverse_kernel, marks, (own, other), [(half, size)] * 2,
        [(size, size), (TILE, TILE)], 40 * size**3, "inverse",
    )


def assemble(at_ref, own_ref, other_ref, full_ref):
    half = own_ref.shape[0]
    full_ref[pl.ds(pl.multiple_of(at_ref[0] * half, half), half), :] = own_ref[...]
    full_ref[pl.ds(pl.multiple_of((1 - at_ref[0]) * half, half), half), :] = other_ref[...]


def left_kernel(
    at_ref, zown_ref, zother_ref, u_ref, uother_ref, f_ref, d_ref, s_ref, dout_ref, sout_ref, z_ref
):
    half = u_ref.shape[0]
    assemble(at_ref, zown_ref, zother_ref, z_ref)
    z = split(z_ref[...])
    own = split(u_ref[...])
    other = split(uother_ref[...])
    inner = ((1,), (0,))
    outer = ((1,), (1,))
    own_at = pl.ds(pl.multiple_of(at_ref[0] * half, half), half)
    other_at = pl.ds(pl.multiple_of((1 - at_ref[0]) * half, half), half)
    for values, base_ref, out_ref in ((own, d_ref, dout_ref), (split(f_ref[...]), s_ref, sout_ref)):
        scaled = split(dot_parts(values, z, inner))
        out_ref[:, own_at] = base_ref[:, own_at] - dot_parts(scaled, own, outer)
        out_ref[:, other_at] = base_ref[:, other_at] - dot_parts(scaled, other, outer)


def right_kernel(
    at_ref, zown_ref, zother_ref, u_ref, f_ref, on_ref, onother_ref, d_ref, s_ref,
    dout_ref, uout_ref, sout_ref, z_ref, full_ref,
):
    half = u_ref.shape[0]
    assemble(at_ref, zown_ref, zother_ref, z_ref)
    assemble(at_ref, on_ref, onother_ref, full_ref)
    z = split(z_ref[...])
    onward = split(full_ref[...])
    inner = ((1,), (0,))
    own_at = pl.ds(pl.multiple_of(at_ref[0] * half, half), half)
    turned = dot_parts(split(full_ref[:, own_at]), z, ((0,), (0,)))
    dout_ref[...] = d_ref[...] - dot_parts(split(turned), onward, inner)
    solved = dot_parts(split(f_ref[...]), z, inner)
    sout_ref[...] = s_ref[...] - dot_parts(split(solved), onward, inner)
    scaled = dot_parts(split(u_ref[...]), z, inner)
    fresh = dot_parts(split(scaled), onward, inner)
    uout_ref[...] = jnp.where(at_ref[1] > 0, -fresh, on_ref[...])


def left(marks, z, zother, u, uother, f, d, s):
    half, size = u.shape
    return call(
        left_kernel, marks, (z, zother, u, uother, f, d, s), [(half, size)] * 2,
        [(size, size)], 12 * size**3, "left",
    )


def right(marks, z, zother, u, f, on, onother, d, s):
    half, size = u.shape
    return call(
        right_kernel, marks, (z, zother, u, f, on, onother, d, s), [(half, size)] * 3,
        [(size, size)] * 2, 18 * size**3, "right",
    )


def swapped(values):
    return lax.ppermute(values, "col", [(0, 1), (1, 0)])


def body(tm_size, diagonal_blocks, upper_blocks, right_sides):
    column = lax.axis_index("col")
    position = lax.axis_index("tm")

    def marks_of(flag):
        return jnp.stack([column, flag.astype(jnp.int32)]).astype(jnp.int32)

    up = [(i, i + 1) for i in range(tm_size - 1)]
    odd_up = [(i, i + 1) for i in range(1, tm_size - 1, 2)]
    odd_down = [(i, i - 1) for i in range(1, tm_size, 2)]

    def to(values, pairs):
        return lax.ppermute(values, "tm", pairs)

    d_even, d_odd = diagonal_blocks[0], diagonal_blocks[1]
    u_even, u_odd = upper_blocks[0], upper_blocks[1]
    f_even, f_odd = right_sides[0], right_sides[1]

    marks = marks_of(position > 0)
    d_other = swapped(d_odd)
    z, z_other = inverse(marks, d_odd, d_other)
    u_left, f_left = to(u_odd, up), to(f_odd, up)
    u_odd_other, u_even_other = swapped(u_odd), swapped(u_even)
    z_left = to(z, up)
    d, s = left(marks, z, z_other, u_odd, u_odd_other, f_odd, d_even, f_even)
    d, u, s = right(
        marks, z_left, swapped(z_left), u_left, f_left, u_even, u_even_other, d, s
    )

    marks = marks_of(jnp.logical_and(position > 0, position % 2 == 0))
    d_other = swapped(d)
    z, _ = inverse(marks, d, d_other)
    u_other = swapped(u)
    u_above, f_above = to(u, odd_down), to(s, odd_down)
    u_above_other = swapped(u_above)
    u_left, f_left = to(u, odd_up), to(s, odd_up)
    z_above, z_left = to(z, odd_down), to(z, odd_up)
    d, s2 = left(marks, z_above, swapped(z_above), u_above, u_above_other, f_above, d, s)
    d, u, s2 = right(marks, z_left, swapped(z_left), u_left, f_left, u, u_other, d, s2)
    return jnp.stack([d, d_odd]), jnp.stack([u, u_odd]), jnp.stack([s2, f_odd])


def solution(mesh):
    placed = (P("tm", "col", None),) * 3
    return jax.shard_map(
        functools.partial(body, mesh.shape["tm"]),
        mesh=mesh,
        in_specs=placed,
        out_specs=placed,
        check_vma=False,
    )
```

```python
import functools

import jax
import jax.numpy as jnp
from jax import lax
from jax.experimental import pallas as pl
from jax.experimental.pallas import tpu as pltpu
from jax.sharding import PartitionSpec as P

LEVELS = 2
TILE = 128
PANEL = 8
F32 = jnp.float32
BF16 = jnp.bfloat16


def split(values):
    high = values.astype(BF16)
    return high, (values - high.astype(F32)).astype(BF16)


def dot_parts(left, right, dims):
    def one(a, b):
        return lax.dot_general(a, b, (dims, ((), ())), preferred_element_type=F32)

    return one(left[0], right[0]) + (one(left[0], right[1]) + one(left[1], right[0]))


def dot3(left, right, dims=((1,), (0,))):
    return dot_parts(split(left), split(right), dims)


def dot6(left, right):
    return jnp.dot(left, right, precision=lax.Precision.HIGHEST, preferred_element_type=F32)


def panel_step(a):
    size = a.shape[0]
    lanes = lax.broadcasted_iota(jnp.int32, (PANEL, size), 1)
    subs = lax.broadcasted_iota(jnp.int32, (PANEL, size), 0)
    cols = [jnp.broadcast_to(a[:, i : i + 1], (size, size)) for i in range(PANEL)]
    rows = [
        jnp.where(
            lanes < PANEL,
            jnp.where(lanes == i, 1.0, 0.0),
            jnp.broadcast_to(a[i : i + 1, :], (PANEL, size)),
        )
        for i in range(PANEL)
    ]
    s = [
        [jnp.broadcast_to(cols[j][i : i + 1, :], (PANEL, size)) if j >= i else None for j in range(PANEL)]
        for i in range(PANEL)
    ]
    scale = [None] * PANEL
    low = {}
    for k in range(PANEL):
        scale[k] = 1.0 / s[k][k]
        for i in range(k + 1, PANEL):
            low[i, k] = s[k][i] * scale[k]
            for j in range(i, PANEL):
                s[i][j] = s[i][j] - low[i, k] * s[k][j]
            rows[i] = rows[i] - low[i, k] * rows[k]
    for k in range(PANEL - 1, -1, -1):
        rows[k] = rows[k] * scale[k]
        for i in range(k):
            pass
    for k in range(PANEL - 1, 0, -1):
        for i in range(k):
            rows[i] = rows[i] - low[k, i] * rows[k]
    solved = rows[0]
    for i in range(1, PANEL):
        solved = jnp.where(subs == i, rows[i], solved)
    pieces = []
    for g in range(1, size // PANEL):
        at = slice(g * PANEL, (g + 1) * PANEL)
        rest = jnp.where(lanes < PANEL, 0.0, a[at])
        first = cols[0][at] * rows[0]
        second = cols[1][at] * rows[1]
        for i in range(2, PANEL, 2):
            first = first + cols[i][at] * rows[i]
            second = second + cols[i + 1][at] * rows[i + 1]
        pieces.append(rest - (first + second))
    pieces.append(solved)
    return pltpu.roll(jnp.concatenate(pieces, axis=0), size - PANEL, axis=1)


INNER = ((1,), (0,))
OUTER = ((1,), (1,))
CHUNKS = 2


def invert(s_ref, tile_ref):
    size = s_ref.shape[0]
    for k in range(0, size, TILE):
        at = slice(k, k + TILE)
        tile_ref[...] = s_ref[at, at]

        @pl.loop(0, TILE // PANEL)
        def _(_step):
            tile_ref[...] = panel_step(tile_ref[...])

        inverse = tile_ref[...]
        row = dot6(inverse, s_ref[at, :])
        s_ref[at, :] = row
        s_ref[at, at] = inverse
        for r in range(0, size, TILE):
            if r != k:
                rat = slice(r, r + TILE)
                column = s_ref[rat, at]
                s_ref[rat, at] = jnp.zeros((TILE, TILE), F32)
                s_ref[rat, :] = s_ref[rat, :] - dot6(column, s_ref[at, :])


def kernel(
    tm_size, d_ref, u_ref, f_ref, dout_ref, uout_ref, fout_ref,
    s_ref, tile_ref, z_ref, full_ref, zown, cur, bufs, send_sem, recv_sem,
):
    half, size = d_ref.shape[1], d_ref.shape[2]
    column = lax.axis_index("col")
    place = lax.axis_index("tm")
    above, below = lax.rem(place + 1, tm_size), lax.rem(place + tm_size - 1, tm_size)
    partner = 1 - column
    odd = lax.rem(place, 2) == 1
    even = lax.rem(place, 2) == 0
    has_left = place > 0
    has_right = place < tm_size - 1
    odd_right = jnp.logical_and(odd, has_right)
    even_left = jnp.logical_and(even, has_left)
    own_at = pl.ds(pl.multiple_of(column * half, half), half)
    other_at = pl.ds(pl.multiple_of(partner * half, half), half)
    rows = half // CHUNKS

    barrier = pltpu.get_barrier_semaphore()

    def greet(where):
        pl.semaphore_signal(barrier, inc=1, device_id=where, device_id_type=pl.DeviceIdType.MESH)

    greet((place, partner))
    pl.when(has_left)(lambda: greet((below, column)))
    pl.when(has_right)(lambda: greet((above, column)))
    pl.semaphore_wait(barrier, 1 + has_left.astype(jnp.int32) + has_right.astype(jnp.int32))

    targets = {"above": (above, column), "below": (below, column), "partner": (place, partner)}

    def copy(slot, source, target, chunk=None):
        sem = CHUNKS * slot + (chunk or 0)
        if chunk is not None:
            at = slice(chunk * rows, (chunk + 1) * rows)
            source, landing = source.at[at], bufs.at[slot, at]
        else:
            landing = bufs.at[slot]
        return pltpu.make_async_remote_copy(
            src_ref=source, dst_ref=landing, send_sem=send_sem.at[sem], recv_sem=recv_sem.at[sem],
            device_id=targets[target], device_id_type=pl.DeviceIdType.MESH,
        )

    def assemble(into, own, other):
        into[own_at, :] = own[...]
        into[other_at, :] = other[...]

    def left(u, uother, f, d, s, dto, sto):
        z = split(z_ref[...])
        own, other = split(u[...]), split(uother[...])
        for values, base, out in ((own, d, dto), (split(f[...]), s, sto)):
            scaled = split(dot_parts(values, z, INNER))
            out[:, own_at] = base[:, own_at] - dot_parts(scaled, own, OUTER)
            out[:, other_at] = base[:, other_at] - dot_parts(scaled, other, OUTER)

    def right(u, f, dto, uto, sto):
        z = split(z_ref[...])
        onward = split(full_ref[...])
        turned = dot_parts(split(full_ref[:, own_at]), z, ((0,), (0,)))
        dto[...] = dto[...] - dot_parts(split(turned), onward, INNER)
        solved = dot_parts(split(f[...]), z, INNER)
        sto[...] = sto[...] - dot_parts(split(solved), onward, INNER)
        scaled = dot_parts(split(u[...]), z, INNER)
        uto[...] = -dot_parts(split(scaled), onward, INNER)

    c_do = copy(0, d_ref.at[1], "partner")
    c_uo = copy(1, u_ref.at[1], "partner")
    c_eo = copy(2, u_ref.at[0], "partner")
    c_ul = copy(3, u_ref.at[1], "above")
    c_fl = copy(4, f_ref.at[1], "above")
    c_zl = [copy(5, zown.at[0], "above", i) for i in range(CHUNKS)]
    c_zlo = [copy(6, bufs.at[5], "partner", i) for i in range(CHUNKS)]
    c_do.start()

    @pl.when(has_right)
    def _():
        c_ul.start()
        c_fl.start()

    c_uo.start()
    c_eo.start()
    c_do.wait_recv()
    assemble(s_ref, d_ref.at[1], bufs.at[0])
    invert(s_ref, tile_ref)
    zown[0] = s_ref[own_at, :]

    @pl.when(has_right)
    def _():
        for i in c_zl:
            i.start()

    c_uo.wait_recv()
    z_ref[...] = s_ref[...]
    left(u_ref.at[1], bufs.at[1], f_ref.at[1], d_ref.at[0], f_ref.at[0], cur.at[0], cur.at[2])
    c_eo.wait_recv()
    cur[1] = u_ref[0]

    @pl.when(has_left)
    def _():
        assemble(full_ref, u_ref.at[0], bufs.at[2])
        c_ul.wait_recv()
        c_fl.wait_recv()
        for i in range(CHUNKS):
            c_zl[i].wait_recv()
            c_zlo[i].start()
        for i in range(CHUNKS):
            c_zlo[i].wait_recv()
        assemble(z_ref, bufs.at[5], bufs.at[6])
        right(bufs.at[3], bufs.at[4], cur.at[0], cur.at[1], cur.at[2])

    c_do1 = copy(7, cur.at[0], "partner")
    c_uo1 = copy(8, cur.at[1], "partner")
    c_ua = copy(9, cur.at[1], "below")
    c_fa = copy(10, cur.at[2], "below")
    c_uao = copy(11, bufs.at[9], "partner")
    c_za = [copy(12, zown.at[1], "below", i) for i in range(CHUNKS)]
    c_zao = [copy(13, bufs.at[12], "partner", i) for i in range(CHUNKS)]
    c_ul1 = copy(14, cur.at[1], "above")
    c_fl1 = copy(15, cur.at[2], "above")
    c_zl1 = [copy(16, zown.at[1], "above", i) for i in range(CHUNKS)]
    c_zl1o = [copy(17, bufs.at[16], "partner", i) for i in range(CHUNKS)]

    @pl.when(odd)
    def _():
        c_do1.start()
        c_ua.start()
        c_fa.start()

        @pl.when(has_right)
        def _():
            c_ul1.start()
            c_fl1.start()

        c_do1.wait_recv()
        assemble(s_ref, cur.at[0], bufs.at[7])
        invert(s_ref, tile_ref)
        zown[1] = s_ref[own_at, :]
        for i in c_za:
            i.start()

        @pl.when(has_right)
        def _():
            for i in c_zl1:
                i.start()

        dout_ref[0] = cur[0]
        uout_ref[0] = cur[1]
        fout_ref[0] = cur[2]

    dout_ref[1] = d_ref[1]
    uout_ref[1] = u_ref[1]
    fout_ref[1] = f_ref[1]

    @pl.when(even)
    def _():
        c_uo1.start()
        c_ua.wait_recv()
        c_uao.start()
        c_uo1.wait_recv()
        assemble(full_ref, cur.at[1], bufs.at[8])
        uout_ref[0] = cur[1]
        c_fa.wait_recv()
        c_uao.wait_recv()
        for i in range(CHUNKS):
            c_za[i].wait_recv()
            c_zao[i].start()
        for i in range(CHUNKS):
            c_zao[i].wait_recv()
        assemble(z_ref, bufs.at[12], bufs.at[13])
        left(bufs.at[9], bufs.at[11], bufs.at[10], cur.at[0], cur.at[2], dout_ref.at[0], fout_ref.at[0])

    @pl.when(even_left)
    def _():
        c_ul1.wait_recv()
        c_fl1.wait_recv()
        for i in range(CHUNKS):
            c_zl1[i].wait_recv()
            c_zl1o[i].start()
        for i in range(CHUNKS):
            c_zl1o[i].wait_recv()
        assemble(z_ref, bufs.at[16], bufs.at[17])
        right(bufs.at[14], bufs.at[15], dout_ref.at[0], uout_ref.at[0], fout_ref.at[0])

    def drained(condition, copies):
        @pl.when(condition)
        def _():
            for i in copies:
                i.wait_send()

    for i in (c_do, c_uo, c_eo):
        i.wait_send()
    drained(has_right, [c_ul, c_fl] + c_zl)
    drained(has_left, c_zlo)
    drained(odd, [c_do1, c_ua, c_fa] + c_za)
    drained(odd_right, [c_ul1, c_fl1] + c_zl1)
    drained(even, [c_uo1, c_uao] + c_zao)
    drained(even_left, c_zl1o)


SLOTS = 18


def body(tm_size, diagonal_blocks, upper_blocks, right_sides):
    shape = diagonal_blocks.shape
    half, size = shape[1], shape[2]
    whole = pl.BlockSpec(memory_space=pltpu.VMEM)
    return pl.pallas_call(
        functools.partial(kernel, tm_size),
        out_shape=[jax.ShapeDtypeStruct(shape, F32)] * 3,
        in_specs=[whole] * 3,
        out_specs=[whole] * 3,
        scratch_shapes=[
            pltpu.VMEM((size, size), F32),
            pltpu.VMEM((TILE, TILE), F32),
            pltpu.VMEM((size, size), F32),
            pltpu.VMEM((size, size), F32),
            pltpu.VMEM((2, half, size), F32),
            pltpu.VMEM((3, half, size), F32),
            pltpu.VMEM((SLOTS, half, size), F32),
            pltpu.SemaphoreType.DMA((SLOTS * CHUNKS,)),
            pltpu.SemaphoreType.DMA((SLOTS * CHUNKS,)),
        ],
        compiler_params=pltpu.CompilerParams(
            vmem_limit_bytes=50 * 2**20, collective_id=0, has_side_effects=True
        ),
        name="reduce_levels",
    )(diagonal_blocks, upper_blocks, right_sides)


def solution(mesh):
    placed = (P("tm", "col", None),) * 3
    return jax.shard_map(
        functools.partial(body, mesh.shape["tm"]),
        mesh=mesh,
        in_specs=placed,
        out_specs=placed,
        check_vma=False,
    )
```

```python
import functools

import jax
import jax.numpy as jnp
from jax import lax
from jax.experimental import pallas as pl
from jax.experimental.pallas import tpu as pltpu
from jax.sharding import PartitionSpec as P

LEVELS = 2
TILE = 128
PANEL = 8
F32 = jnp.float32
BF16 = jnp.bfloat16


def split(values):
    high = values.astype(BF16)
    return high, (values - high.astype(F32)).astype(BF16)


def dot_parts(left, right, dims):
    def one(a, b):
        return lax.dot_general(a, b, (dims, ((), ())), preferred_element_type=F32)

    return one(left[0], right[0]) + (one(left[0], right[1]) + one(left[1], right[0]))


def dot3(left, right, dims=((1,), (0,))):
    return dot_parts(split(left), split(right), dims)


def panel_step(a, p):
    size = a[0].shape[1]
    count = size // PANEL
    base = PANEL * p
    lanes = lax.broadcasted_iota(jnp.int32, (PANEL, size), 1)
    subs = lax.broadcasted_iota(jnp.int32, (PANEL, size), 0)
    inside = jnp.logical_and(lanes >= base, lanes < base + PANEL)

    def spread(values, i):
        return jnp.broadcast_to(values[:, base + i : base + i + 1], (PANEL, size))

    head = [spread(a[p], i) for i in range(PANEL)]
    s = [
        [jnp.broadcast_to(head[j][i : i + 1, :], (PANEL, size)) if j >= i else None for j in range(PANEL)]
        for i in range(PANEL)
    ]
    rows = [
        jnp.where(
            inside,
            jnp.where(lanes == base + i, 1.0, 0.0),
            jnp.broadcast_to(a[p][i : i + 1, :], (PANEL, size)),
        )
        for i in range(PANEL)
    ]
    scale = [None] * PANEL
    low = {}
    for k in range(PANEL):
        scale[k] = 1.0 / s[k][k]
        for i in range(k + 1, PANEL):
            low[i, k] = s[k][i] * scale[k]
            for j in range(i, PANEL):
                s[i][j] = s[i][j] - low[i, k] * s[k][j]
            rows[i] = rows[i] - low[i, k] * rows[k]
    for k in range(PANEL):
        rows[k] = rows[k] * scale[k]
    for k in range(PANEL - 1, 0, -1):
        for i in range(k):
            rows[i] = rows[i] - low[k, i] * rows[k]
    solved = rows[0]
    for i in range(1, PANEL):
        solved = jnp.where(subs == i, rows[i], solved)
    fresh = [None] * count
    fresh[p] = solved
    for step in range(1, count):
        g = (p + step) % count
        col = [spread(a[g], i) for i in range(PANEL)]
        terms = [col[i] * rows[i] for i in range(PANEL)]
        while len(terms) > 1:
            terms = [terms[i] + terms[i + 1] for i in range(0, len(terms), 2)]
        fresh[g] = jnp.where(inside, 0.0, a[g]) - terms[0]
    return fresh


INNER = ((1,), (0,))
OUTER = ((1,), (1,))
CHUNKS = 4


def invert(s_ref, tile_ref):
    size = s_ref.shape[0]
    blocks = size // TILE

    @pl.loop(0, blocks)
    def _(k):
        at = pl.ds(pl.multiple_of(k * TILE, TILE), TILE)
        groups = [
            s_ref[pl.ds(pl.multiple_of(k * TILE, TILE) + PANEL * g, PANEL), at]
            for g in range(TILE // PANEL)
        ]
        for p in range(TILE // PANEL):
            groups = panel_step(groups, p)
        for g in range(TILE // PANEL):
            tile_ref[PANEL * g : PANEL * (g + 1), :] = groups[g]
        inverse = tile_ref[...]
        row = dot3(inverse, s_ref[at, :])
        s_ref[at, :] = row
        s_ref[at, at] = inverse
        row_parts = split(s_ref[at, :])
        for r in range(blocks):

            @pl.when(r != k)
            def _():
                rat = slice(r * TILE, (r + 1) * TILE)
                column = s_ref[rat, at]
                s_ref[rat, at] = jnp.zeros((TILE, TILE), F32)
                s_ref[rat, :] = s_ref[rat, :] - dot_parts(split(column), row_parts, INNER)


def kernel(
    tm_size, d_ref, u_ref, f_ref, dout_ref, uout_ref, fout_ref,
    s_ref, tile_ref, z_ref, full_ref, zown, cur, bufs, send_sem, recv_sem,
):
    half, size = d_ref.shape[1], d_ref.shape[2]
    column = lax.axis_index("col")
    place = lax.axis_index("tm")
    above, below = lax.rem(place + 1, tm_size), lax.rem(place + tm_size - 1, tm_size)
    over, under = lax.rem(place + 2, tm_size), lax.rem(place + tm_size - 2, tm_size)
    partner = 1 - column
    odd = lax.rem(place, 2) == 1
    even = lax.rem(place, 2) == 0
    has_left = place > 0
    has_right = place < tm_size - 1
    even_left = jnp.logical_and(even, has_left)
    even_right = jnp.logical_and(even, place < tm_size - 2)
    own_at = pl.ds(pl.multiple_of(column * half, half), half)
    other_at = pl.ds(pl.multiple_of(partner * half, half), half)
    rows = half // CHUNKS

    barrier = pltpu.get_barrier_semaphore()

    def greet(where):
        pl.semaphore_signal(barrier, inc=1, device_id=where, device_id_type=pl.DeviceIdType.MESH)

    greet((place, partner))
    pl.when(has_left)(lambda: greet((below, column)))
    pl.when(has_right)(lambda: greet((above, column)))
    pl.when(even_left)(lambda: greet((under, column)))
    pl.when(even_right)(lambda: greet((over, column)))
    peers = [x.astype(jnp.int32) for x in (has_left, has_right, even_left, even_right)]
    pl.semaphore_wait(barrier, 1 + peers[0] + peers[1] + peers[2] + peers[3])

    targets = {"above": (above, column), "below": (below, column), "partner": (place, partner), "over": (over, column)}

    def copy(slot, source, target, chunk=None):
        sem = CHUNKS * slot + (chunk or 0)
        if chunk is not None:
            at = slice(chunk * rows, (chunk + 1) * rows)
            source, landing = source.at[at], bufs.at[slot, at]
        else:
            landing = bufs.at[slot]
        return pltpu.make_async_remote_copy(
            src_ref=source, dst_ref=landing, send_sem=send_sem.at[sem], recv_sem=recv_sem.at[sem],
            device_id=targets[target], device_id_type=pl.DeviceIdType.MESH,
        )

    def assemble(into, own, other):
        into[own_at, :] = own[...]
        into[other_at, :] = other[...]

    def left(u, uother, f, d, s, dto, sto):
        z = split(z_ref[...])
        own, other = split(u[...]), split(uother[...])
        for values, base, out in ((own, d, dto), (split(f[...]), s, sto)):
            scaled = split(dot_parts(values, z, INNER))
            out[:, own_at] = base[:, own_at] - dot_parts(scaled, own, OUTER)
            out[:, other_at] = base[:, other_at] - dot_parts(scaled, other, OUTER)

    def right(u, f, dto, uto, sto):
        z = split(z_ref[...])
        onward = split(full_ref[...])
        turned = dot_parts(split(full_ref[:, own_at]), z, ((0,), (0,)))
        dto[...] = dto[...] - dot_parts(split(turned), onward, INNER)
        solved = dot_parts(split(f[...]), z, INNER)
        sto[...] = sto[...] - dot_parts(split(solved), onward, INNER)
        scaled = dot_parts(split(u[...]), z, INNER)
        uto[...] = -dot_parts(split(scaled), onward, INNER)

    c_do = copy(0, d_ref.at[1], "partner")
    c_uo = copy(1, u_ref.at[1], "partner")
    c_eo = copy(2, u_ref.at[0], "partner")
    c_ul = copy(3, u_ref.at[1], "above")
    c_fl = copy(4, f_ref.at[1], "above")
    c_zl = [copy(5, zown.at[0], "above", i) for i in range(CHUNKS)]
    c_zlo = [copy(6, bufs.at[5], "partner", i) for i in range(CHUNKS)]
    c_do.start()

    @pl.when(has_right)
    def _():
        c_ul.start()
        c_fl.start()

    c_uo.start()
    c_eo.start()
    c_do.wait_recv()
    assemble(s_ref, d_ref.at[1], bufs.at[0])
    invert(s_ref, tile_ref)
    zown[0] = s_ref[own_at, :]

    @pl.when(has_right)
    def _():
        for i in c_zl:
            i.start()

    c_uo.wait_recv()
    z_ref[...] = s_ref[...]
    left(u_ref.at[1], bufs.at[1], f_ref.at[1], d_ref.at[0], f_ref.at[0], cur.at[0], cur.at[2])
    c_eo.wait_recv()
    cur[1] = u_ref[0]

    @pl.when(has_left)
    def _():
        assemble(full_ref, u_ref.at[0], bufs.at[2])
        c_ul.wait_recv()
        c_fl.wait_recv()
        for i in range(CHUNKS):
            c_zl[i].wait_recv()
            c_zlo[i].start()
        for i in range(CHUNKS):
            c_zlo[i].wait_recv()
        assemble(z_ref, bufs.at[5], bufs.at[6])
        right(bufs.at[3], bufs.at[4], cur.at[0], cur.at[1], cur.at[2])

    c_do1 = copy(7, cur.at[0], "partner")
    c_uo1 = copy(8, cur.at[1], "partner")
    c_ua = copy(9, cur.at[1], "below")
    c_fa = copy(10, cur.at[2], "below")
    c_uao = copy(11, bufs.at[9], "partner")
    c_za = [copy(12, zown.at[1], "below", i) for i in range(CHUNKS)]
    c_zao = [copy(13, bufs.at[12], "partner", i) for i in range(CHUNKS)]
    c_ul1 = copy(14, bufs.at[9], "over")
    c_fl1 = copy(15, bufs.at[10], "over")
    c_zl1 = [copy(16, bufs.at[12], "over", i) for i in range(CHUNKS)]
    c_zl1o = [copy(17, bufs.at[16], "partner", i) for i in range(CHUNKS)]

    @pl.when(odd)
    def _():
        c_do1.start()
        c_ua.start()
        c_fa.start()
        c_do1.wait_recv()
        assemble(s_ref, cur.at[0], bufs.at[7])
        invert(s_ref, tile_ref)
        zown[1] = s_ref[own_at, :]
        for i in c_za:
            i.start()

        dout_ref[0] = cur[0]
        uout_ref[0] = cur[1]
        fout_ref[0] = cur[2]

    dout_ref[1] = d_ref[1]
    uout_ref[1] = u_ref[1]
    fout_ref[1] = f_ref[1]

    @pl.when(even)
    def _():
        c_uo1.start()
        c_ua.wait_recv()
        pl.when(even_right)(c_ul1.start)
        c_uao.start()
        c_uo1.wait_recv()
        assemble(full_ref, cur.at[1], bufs.at[8])
        uout_ref[0] = cur[1]
        c_fa.wait_recv()
        pl.when(even_right)(c_fl1.start)
        c_uao.wait_recv()
        for i in range(CHUNKS):
            c_za[i].wait_recv()
            pl.when(even_right)(c_zl1[i].start)
            c_zao[i].start()
        for i in range(CHUNKS):
            c_zao[i].wait_recv()
        assemble(z_ref, bufs.at[12], bufs.at[13])
        left(bufs.at[9], bufs.at[11], bufs.at[10], cur.at[0], cur.at[2], dout_ref.at[0], fout_ref.at[0])

    @pl.when(even_left)
    def _():
        c_ul1.wait_recv()
        c_fl1.wait_recv()
        for i in range(CHUNKS):
            c_zl1[i].wait_recv()
            c_zl1o[i].start()
        for i in range(CHUNKS):
            c_zl1o[i].wait_recv()
        assemble(z_ref, bufs.at[16], bufs.at[17])
        right(bufs.at[14], bufs.at[15], dout_ref.at[0], uout_ref.at[0], fout_ref.at[0])

    def drained(condition, copies):
        @pl.when(condition)
        def _():
            for i in copies:
                i.wait_send()

    for i in (c_do, c_uo, c_eo):
        i.wait_send()
    drained(has_right, [c_ul, c_fl] + c_zl)
    drained(has_left, c_zlo)
    drained(odd, [c_do1, c_ua, c_fa] + c_za)
    drained(even_right, [c_ul1, c_fl1] + c_zl1)
    drained(even, [c_uo1, c_uao] + c_zao)
    drained(even_left, c_zl1o)


SLOTS = 18


def body(tm_size, diagonal_blocks, upper_blocks, right_sides):
    shape = diagonal_blocks.shape
    half, size = shape[1], shape[2]
    whole = pl.BlockSpec(memory_space=pltpu.VMEM)
    return pl.pallas_call(
        functools.partial(kernel, tm_size),
        out_shape=[jax.ShapeDtypeStruct(shape, F32)] * 3,
        in_specs=[whole] * 3,
        out_specs=[whole] * 3,
        scratch_shapes=[
            pltpu.VMEM((size, size), F32),
            pltpu.VMEM((TILE, TILE), F32),
            pltpu.VMEM((size, size), F32),
            pltpu.VMEM((size, size), F32),
            pltpu.VMEM((2, half, size), F32),
            pltpu.VMEM((3, half, size), F32),
            pltpu.VMEM((SLOTS, half, size), F32),
            pltpu.SemaphoreType.DMA((SLOTS * CHUNKS,)),
            pltpu.SemaphoreType.DMA((SLOTS * CHUNKS,)),
        ],
        compiler_params=pltpu.CompilerParams(
            vmem_limit_bytes=50 * 2**20, collective_id=0, has_side_effects=True
        ),
        name="reduce_levels",
    )(diagonal_blocks, upper_blocks, right_sides)


def solution(mesh):
    placed = (P("tm", "col", None),) * 3
    return jax.shard_map(
        functools.partial(body, mesh.shape["tm"]),
        mesh=mesh,
        in_specs=placed,
        out_specs=placed,
        check_vma=False,
    )
```
